32 devices in a mesh: groups: 2 (over x), tile: 16 (over z, y, core).
Axes of the slice: x: 2, y: 2, z: 4, core: 2. Of those that a mesh axis runs over, the one named last changes fastest.
Arguments:
- reference_feat: float32 [8, 1024, 256], P('groups', 'tile'), parts along dimension 0, may hold values from -32 to 32
- secondary_feat: float32 [4, 4, 1024, 256], P('groups', None, 'tile'), parts along dimension 0, may hold values from -32 to 32
- pair_offsets: int32 [4, 16], P('groups', 'tile'), parts along dimension 0, may hold values from 0 to 63, as said below
- w_query_key: float32 [256, 64], replicated, may hold values from -0.375 to 0.375
- w_value: float32 [256, 64], replicated, may hold values from -0.375 to 0.375
- conv_first: float32 [8, 8, 3, 3, 3], replicated, may hold values from -0.8 to 0.8
- conv_second: float32 [8, 8, 3, 3, 3], replicated, may hold values from -0.4 to 0.4
Outputs:
- disparity: float32 [8, 1024], P('groups', 'tile'), parts along dimension 0
The draws below stay inside these ranges and needn't reach their ends.
There are 2 independent parts, one for each index of `groups`. The reference program is written for one: setup_inputs(seed, part) draws one part's arguments, and reference() takes and returns one part's arrays. A program takes and returns all parts, laid end to end along the dimension named above; an argument that names none is the same for every part. Nothing has to cross between parts.
Inputs may be any that keep to these rules, and one draw needn't show every extreme that they name: `pair_offsets`: in each pair's row some tile holds 63 and the next tile, cyclically, holds 0.
All inputs are finite; a program needn't handle non-finite values.
Results may differ from the reference program's by a relative error of at most 0.0003.
Values sent between devices are 32-bit elements; how exact they have to be, the bound alone decides.
A program may use at most 192 MiB of HBM per device.

```python
from functools import reduce
import jax
import jax.numpy as jnp
from jax import lax

F = 256
CH = 64
CORR_GROUPS = 8
CONV_CH = 8
DISP = 128
RAD = 3
TW = 64
ROWS = 4
PAIRS = 2
NTILES = 16
NX = 1024


def spiked_draw(key, shape):
    base_key = jax.random.fold_in(key, 0)
    values = jax.random.normal(base_key, shape, jnp.float32)
    return jnp.clip(values, -6.0, 6.0)


def draw_reference_feat(key, part):
    return spiked_draw(jax.random.fold_in(key, 11), (ROWS, NX, F))


def draw_secondary_feat(key, part):
    return spiked_draw(jax.random.fold_in(key, 23), (PAIRS, ROWS, NX, F))


def draw_pair_offsets(key, part):
    base_key, peak_key = jax.random.split(jax.random.fold_in(key, 37))
    offset_table = jax.random.randint(base_key, (PAIRS, NTILES), 0, TW)
    peak_at = jax.random.randint(peak_key, (PAIRS, 1), 0, NTILES)
    positions = jnp.arange(NTILES)[None, :]
    offset_table = jnp.where(positions == peak_at, TW - 1, offset_table)
    offset_table = jnp.where(positions == (peak_at + 1) % NTILES, 0, offset_table)
    return offset_table.astype(jnp.int32)


def centred(own_key, extent, scale, bound, kind=jnp.bfloat16):
    result = scale * jax.random.normal(own_key, extent, jnp.float32)
    return jnp.clip(result, min=-bound, max=bound).astype(kind)


def setup_inputs(seed: int = 0, part: int = 0) -> dict:
    arg_keys = jax.random.split(jax.random.key(seed), 8)
    own_keys = jax.random.split(jax.random.fold_in(arg_keys[7], part), 8)
    reference_feat = draw_reference_feat(jax.random.fold_in(jax.random.fold_in(arg_keys[7], part), 71), part)
    secondary_feat = draw_secondary_feat(jax.random.fold_in(jax.random.fold_in(arg_keys[7], part), 71), part)
    pair_offsets = draw_pair_offsets(jax.random.fold_in(jax.random.fold_in(arg_keys[7], part), 71), part)
    w_query_key = centred(arg_keys[3], (F, CH), F ** -0.5, 0.375, jnp.float32)
    w_value = centred(arg_keys[4], (F, CH), F ** -0.5, 0.375, jnp.float32)
    conv_first = centred(arg_keys[5], (CONV_CH, CORR_GROUPS, 3, 3, 3), 0.2, 0.8, jnp.float32)
    conv_second = centred(arg_keys[6], (CONV_CH, CONV_CH, 3, 3, 3), 0.1, 0.4, jnp.float32)
    return dict(reference_feat=reference_feat, secondary_feat=secondary_feat, pair_offsets=pair_offsets, w_query_key=w_query_key, w_value=w_value, conv_first=conv_first, conv_second=conv_second)


precise = lax.Precision.HIGHEST


def window_attention(query_key, value_proj, widened, row_valid, col_valid, channels):
    row_count = query_key.shape[1]
    col_count = query_key.shape[2]
    scores = []
    for row_step in range(3):
        for col_step in range(2 * RAD + 1):
            keys_here = widened[:, row_step:row_step + row_count, col_step:col_step + col_count, :channels]
            allowed = row_valid[row_step:row_step + row_count][:, None] & col_valid[col_step:col_step + col_count][None, :]
            raw_score = jnp.sum(query_key * keys_here, axis=-1) / channels
            scores.append(jnp.where(allowed[None], raw_score, -1e30))
    row_peak = reduce(jnp.maximum, scores)
    weights = [jnp.exp(score_one - row_peak) for score_one in scores]
    exp_sum = reduce(jnp.add, weights)
    mixed = jnp.zeros(value_proj.shape, jnp.float32)
    position = 0
    for row_step in range(3):
        for col_step in range(2 * RAD + 1):
            vals_here = widened[:, row_step:row_step + row_count, col_step:col_step + col_count, channels:]
            mixed = mixed + weights[position][..., None] * vals_here
            position = position + 1
    return value_proj + mixed / exp_sum[..., None]


def attend(images, w_query_key, w_value):
    query_key = jnp.einsum('vrxf,fc->vrxc', images, w_query_key, precision=precise)
    value_proj = jnp.einsum('vrxf,fc->vrxc', images, w_value, precision=precise)
    channels = query_key.shape[-1]
    row_count = images.shape[1]
    col_count = images.shape[2]
    joined = jnp.concatenate([query_key, value_proj], axis=-1)
    widened = jnp.pad(joined, ((0, 0), (1, 1), (RAD, RAD), (0, 0)))
    row_ids = jnp.arange(row_count + 2)
    col_ids = jnp.arange(col_count + 2 * RAD)
    row_valid = (row_ids >= 1) & (row_ids <= row_count)
    col_valid = (col_ids >= RAD) & (col_ids < col_count + RAD)
    return window_attention(query_key, value_proj, widened, row_valid, col_valid, channels)


def correlate(left_feat, right_feat, shifts):
    row_count = left_feat.shape[0]
    channels = left_feat.shape[2]
    group_size = channels // CORR_GROUPS
    padded = jnp.pad(right_feat, ((0, 0), (0, TW + DISP), (0, 0)))
    grouped_left = left_feat.reshape(row_count, NTILES, TW, CORR_GROUPS, group_size)
    spread = jnp.arange(TW)[:, None] + jnp.arange(DISP)[None, :]

    def one_tile(tile_pos):
        start = (tile_pos * TW + shifts[tile_pos]).astype(jnp.int32)
        window = lax.dynamic_slice_in_dim(padded, start, TW + DISP - 1, 1)
        taken_cols = window[:, spread, :].reshape(row_count, TW, DISP, CORR_GROUPS, group_size)
        left_tile = lax.dynamic_index_in_dim(grouped_left, tile_pos, 1, keepdims=False)
        return jnp.sum(left_tile[:, :, None] * taken_cols, axis=-1) / group_size

    volume = lax.map(one_tile, jnp.arange(NTILES, dtype=jnp.int32))
    volume = jnp.transpose(volume, (4, 1, 0, 2, 3))
    return volume.reshape(CORR_GROUPS, row_count, NTILES * TW, DISP)


def filter_costs(volume, conv_first, conv_second):
    conv_layout = ('NCHWD', 'OIHWD', 'NCHWD')
    first_out = jax.nn.relu(lax.conv_general_dilated(volume[None], conv_first, (1, 1, 1), ((1, 1), (1, 1), (1, 1)), dimension_numbers=conv_layout, precision=precise))
    second_out = jax.nn.relu(lax.conv_general_dilated(first_out, conv_second, (1, 1, 1), ((1, 1), (1, 1), (1, 1)), dimension_numbers=conv_layout, precision=precise))
    return jnp.sum(second_out[0], axis=0)


def reference(reference_feat, secondary_feat, pair_offsets, w_query_key, w_value, conv_first, conv_second):
    images = jnp.concatenate([reference_feat[None], secondary_feat], axis=0)
    features = attend(images, w_query_key, w_value)
    score_sum = jnp.zeros((reference_feat.shape[0], reference_feat.shape[1], DISP), jnp.float32)
    for pair_pos in range(PAIRS):
        volume = correlate(features[0], features[pair_pos + 1], pair_offsets[pair_pos])
        score_sum = score_sum + filter_costs(volume, conv_first, conv_second)
    row_peak = jnp.max(score_sum, axis=-1, keepdims=True)
    disp_prob = jnp.exp(score_sum - row_peak)
    disp_prob = disp_prob / jnp.sum(disp_prob, axis=-1, keepdims=True)
    levels = jnp.arange(DISP, dtype=jnp.float32)
    return jnp.sum(disp_prob * levels, axis=-1) / DISP
```

```python
import functools

import jax
import jax.numpy as jnp
from jax import lax
from jax.experimental import pallas as pl
from jax.experimental.pallas import tpu as pltpu
from jax.sharding import PartitionSpec as P

GROUPS = 8
DISP = 128
RAD = 3
ROWS = 4
CH = 64
LANES = ROWS * CH
HALO = 8
F32 = jnp.float32
BF16 = jnp.bfloat16


def dot(a, b):
    return jnp.dot(a, b, preferred_element_type=F32)


def split2(x):
    hi = x.astype(BF16)
    return hi, (x - hi.astype(F32)).astype(BF16)


def split3(x):
    hi = x.astype(BF16)
    rest = x - hi.astype(F32)
    mid = rest.astype(BF16)
    return hi, mid, (rest - mid.astype(F32)).astype(BF16)


def attend_kernel(images, width, info, ref, sec, left, right, wq, wv, out_ref, out_sec, out_halo, stacked, weights, query, value, scores):
    wide = width + 2 * HALO
    first_col, total_cols = info[0], info[1]
    weights[:, :CH] = wq[...]
    weights[:, CH:] = wv[...]
    zeros = jnp.zeros((HALO, LANES), F32)
    for image in range(images):
        for row in range(ROWS):
            base = row * wide
            stacked[base:base + HALO, :] = left[image, row]
            stacked[base + HALO:base + HALO + width, :] = ref[row] if image == 0 else sec[image - 1, row]
            stacked[base + HALO + width:base + wide, :] = right[image, row]
        both = jnp.dot(stacked[...], weights[...], precision=lax.Precision.HIGHEST, preferred_element_type=F32)
        for row in range(ROWS):
            part = both[row * wide:(row + 1) * wide, :]
            query[HALO:HALO + wide, row * CH:(row + 1) * CH] = part[:, :CH]
            value[HALO:HALO + wide, row * CH:(row + 1) * CH] = part[:, CH:]
        for buffer in (query, value):
            buffer[0:HALO, :] = zeros
            buffer[HALO + wide:, :] = zeros
        lane_row = lax.broadcasted_iota(jnp.int32, (wide, LANES), 1) // CH
        column = lax.broadcasted_iota(jnp.int32, (wide, LANES), 0) + (first_col - HALO)
        ones = jnp.where(
            lax.broadcasted_iota(jnp.int32, (LANES, LANES), 0) // CH
            == lax.broadcasted_iota(jnp.int32, (LANES, LANES), 1) // CH,
            1.0 / CH, 0.0).astype(BF16)
        own = query[HALO:HALO + wide, :]
        peak = jnp.full((wide, LANES), -1e30, F32)
        place = 0
        for shift in range(-RAD, RAD + 1):
            keys = query[HALO + shift:HALO + shift + wide, :]
            col_ok = (column + shift >= 0) & (column + shift < total_cols)
            for step in (-1, 0, 1):
                moved = pltpu.roll(keys, (-step * CH) % LANES, 1) if step else keys
                hi, mid, low = split3(own * moved)
                score = dot(hi, ones) + dot(mid, ones) + dot(low, ones)
                row_ok = (lane_row + step >= 0) & (lane_row + step < ROWS)
                score = jnp.where(col_ok & row_ok, score, -1e30)
                scores[place] = score
                peak = jnp.maximum(peak, score)
                place += 1
        total = jnp.zeros((wide, LANES), F32)
        mixed = jnp.zeros((wide, LANES), F32)
        place = 0
        for shift in range(-RAD, RAD + 1):
            vals = value[HALO + shift:HALO + shift + wide, :]
            for step in (-1, 0, 1):
                moved = pltpu.roll(vals, (-step * CH) % LANES, 1) if step else vals
                weight = jnp.exp(scores[place] - peak)
                total = total + weight
                mixed = mixed + weight * moved
                place += 1
        feature = value[HALO:HALO + wide, :] + mixed / total
        if image == 0:
            out_ref[...] = jnp.where((column >= 0) & (column < total_cols), feature, 0.0)
        else:
            out_halo[image - 1] = feature[:HALO]
            out_sec[image - 1] = feature[HALO:HALO + width]


def cost_kernel(pairs, width, info, taps, feat, halo, sec0, sec1, sec2, sec3, out,
                window, moved, padded, prod, plane, high, low, w_high, w_low):
    group = ROWS * GROUPS
    blocks = width // 8
    block = 8 * group
    span = 10 * group
    full = (width + 4) * group
    tail = blocks * block
    tiles = DISP + 16
    window[...] = jnp.zeros_like(window)
    for pair in range(pairs):
        window[pair, 0:HALO, :] = halo[pair]
        for place, sec in enumerate((sec0, sec1, sec2, sec3)):
            window[pair, HALO + place * width:HALO + (place + 1) * width, :] = sec[pair]
        plane[pair, 0:8, :] = jnp.zeros((8, full), F32)
        plane[pair, 8 + DISP:, :] = jnp.zeros((8, full), F32)
    padded[...] = jnp.zeros_like(padded)
    padded[0:width + 2 * HALO, :] = feat[...]
    for conv in range(2):
        for tap in range(3):
            w_high[conv, tap] = jnp.zeros((span, block), BF16)
            w_low[conv, tap] = jnp.zeros((span, block), BF16)
            hi, lo = split2(taps[conv, tap])
            for col in range(8):
                at = (slice(col * group, (col + 3) * group), slice(col * group, (col + 1) * group))
                w_high[(conv, tap) + at] = hi
                w_low[(conv, tap) + at] = lo
    feat_hi, feat_lo = split2(padded[...].T)
    lane = lax.broadcasted_iota(jnp.int32, (DISP, 128), 1)

    def left_matrix(at):
        rows = lax.broadcasted_iota(jnp.int32, (128, block), 0)
        lanes = lax.broadcasted_iota(jnp.int32, (128, block), 1)
        spread = jnp.where(rows == lanes // group + (8 * at + HALO - 2), 1.0, 0.0).astype(BF16)
        keep = jnp.where(
            lax.broadcasted_iota(jnp.int32, (LANES, block), 0) // GROUPS
            == lax.broadcasted_iota(jnp.int32, (LANES, block), 1) % group,
            1.0 / (CH // GROUPS), 0.0)
        return (dot(feat_hi, spread) * keep).astype(BF16), (dot(feat_lo, spread) * keep).astype(BF16)

    def shifted(pair, offset, start, count):
        first = offset + (HALO - 2)
        rest = first % 8
        aligned = pl.multiple_of(first - rest + start, 8)
        rows = window[pair, pl.ds(aligned, count + 8), :]
        return pltpu.roll(rows, count + 8 - rest, 0)[:count]

    def skewed(rows, left_hi, left_lo, halves):
        right_hi, right_lo = split2(rows)
        prod[...] = dot(right_hi, left_hi) + dot(right_hi, left_lo) + dot(right_lo, left_hi)
        result = []
        for half in range(halves):
            lanes = slice(half * 128, (half + 1) * 128)
            value = prod[half * 4:half * 4 + DISP, lanes]
            for col in range(1, 4):
                other = prod[half * 4 + col:half * 4 + col + DISP, lanes]
                value = jnp.where(lane >= col * group, other, value)
            result.append(value)
        return result

    for pair in range(pairs):
        moved[pair] = shifted(pair, info[3 * pair], 0, width + tiles)

    def volume_step(at, carry):
        left_hi, left_lo = left_matrix(at)
        for pair in range(pairs):
            parts = skewed(moved[pair, pl.ds(pl.multiple_of(8 * at, 8), tiles), :], left_hi, left_lo, 2)
            for half in range(2):
                plane[pair, 8:8 + DISP, pl.ds(pl.multiple_of(at * block + half * 128, 128), 128)] = parts[half]
        return carry

    lax.fori_loop(0, blocks, volume_step, 0)
    left_hi, left_lo = left_matrix(0)
    for pair in range(pairs):
        (edge,) = skewed(shifted(pair, info[3 * pair + 1], 0, tiles), left_hi, left_lo, 1)
        plane[pair, 8:8 + DISP, 0:128] = jnp.where(lane < 2 * group, edge, plane[pair, 8:8 + DISP, 0:128])
    left_hi, left_lo = left_matrix(blocks)
    for pair in range(pairs):
        (mine,) = skewed(moved[pair, width:width + tiles, :], left_hi, left_lo, 1)
        (edge,) = skewed(shifted(pair, info[3 * pair + 2], width, tiles), left_hi, left_lo, 1)
        plane[pair, 8:8 + DISP, tail:tail + 128] = jnp.where(lane < 2 * group, mine, edge)

    def split_planes():
        def step(at, carry):
            lanes = pl.ds(pl.multiple_of(at * 128, 128), 128)
            for pair in range(pairs):
                for tap in range(3):
                    hi, lo = split2(plane[pair, 7 + tap:7 + tap + DISP, lanes])
                    high[tap, pair * DISP:(pair + 1) * DISP, lanes] = hi
                    low[tap, pair * DISP:(pair + 1) * DISP, lanes] = lo
            return carry

        lax.fori_loop(0, full // 128, step, 0)

    def conv(which, start, depth, count):
        total = None
        lanes = pl.ds(start, depth)
        for tap in range(3):
            hi = high[tap, :, lanes]
            lo = low[tap, :, lanes]
            wh = w_high[which, tap, 0:depth, 0:count]
            wl = w_low[which, tap, 0:depth, 0:count]
            term = dot(hi, wh) + dot(hi, wl) + dot(lo, wh)
            total = term if total is None else total + term
        return jnp.maximum(total, 0.0)

    split_planes()
    is_first, is_last = info[3 * pairs], info[3 * pairs + 1]

    def first_step(at, carry):
        start = pl.multiple_of(at * block, block)
        result = conv(0, start, span, block)
        lanes = lax.broadcasted_iota(jnp.int32, result.shape, 1)
        result = jnp.where((lanes < group) & (is_first + jnp.where(at == 0, 1, 0) == 2), 0.0, result)
        for pair in range(pairs):
            plane[pair, 8:8 + DISP, pl.ds(start, block)] = result[pair * DISP:(pair + 1) * DISP]
        return carry

    lax.fori_loop(0, blocks, first_step, 0)
    result = conv(0, tail, 128, 128)
    lanes = lax.broadcasted_iota(jnp.int32, result.shape, 1)
    result = jnp.where((lanes >= group) & (is_last == 1), 0.0, result)
    for pair in range(pairs):
        plane[pair, 8:8 + DISP, tail:tail + 128] = result[pair * DISP:(pair + 1) * DISP]
    split_planes()
    level = lax.broadcasted_iota(jnp.int32, (DISP, block), 0).astype(F32)

    def second_step(at, carry):
        result = conv(1, pl.multiple_of(at * block, block), span, block)
        score = result[:DISP]
        for pair in range(1, pairs):
            score = score + result[pair * DISP:(pair + 1) * DISP]
        for shift in (4, 2, 1):
            score = score + pltpu.roll(score, block - shift, 1)
        weight = jnp.exp(score - jnp.max(score, axis=0, keepdims=True))
        mean = jnp.sum(weight * level, axis=0, keepdims=True) / jnp.sum(weight, axis=0, keepdims=True)
        out[pl.ds(at, 1), :] = mean / DISP
        return carry

    lax.fori_loop(0, blocks, second_step, 0)


def passed_along(value, axis, steps):
    count = lax.axis_size(axis)
    first, last = (max(0, -steps), min(count, count - steps))
    return lax.ppermute(value, axis, [(source, source + steps) for source in range(first, last)])


def tap_matrices(conv_first, conv_second):
    both = jnp.stack([conv_first, conv_second])
    flipped = jnp.transpose(both, (0, 5, 4, 3, 2, 1))
    rows = jnp.pad(flipped, ((0, 0), (0, 0), (0, 0), (ROWS - 1, ROWS - 1), (0, 0), (0, 0)))
    parts = [rows[:, :, :, ROWS - out:2 * ROWS - out] for out in range(ROWS)]
    joined = jnp.concatenate(parts, axis=-1)
    return joined.reshape(2, 3, 3 * ROWS * GROUPS, ROWS * GROUPS)


def on_device(reference_feat, secondary_feat, pair_offsets, w_query_key, w_value, conv_first, conv_second):
    pairs = secondary_feat.shape[0]
    images = pairs + 1
    width = reference_feat.shape[1]
    tile_id = lax.axis_index("tile")
    count = lax.axis_size("tile")
    wide = width + 2 * HALO
    group = ROWS * GROUPS
    full = (width + 4) * group
    vmem = pl.BlockSpec(memory_space=pltpu.VMEM)
    smem = pl.BlockSpec(memory_space=pltpu.SMEM)
    ends = jnp.concatenate([reference_feat[None, :, -HALO:], secondary_feat[:, :, -HALO:]], axis=0)
    starts = jnp.concatenate([reference_feat[None, :, :HALO], secondary_feat[:, :, :HALO]], axis=0)
    left = passed_along(ends, "tile", 1)
    right = passed_along(starts, "tile", -1)
    before = passed_along(pair_offsets, "tile", 1)
    after = passed_along(pair_offsets, "tile", -1)
    taps = tap_matrices(conv_first, conv_second)
    place = jnp.stack([tile_id * width, count * width]).astype(jnp.int32)
    feat, own, halo = pl.pallas_call(
        functools.partial(attend_kernel, images, width),
        out_shape=(
            jax.ShapeDtypeStruct((wide, LANES), F32),
            jax.ShapeDtypeStruct((pairs, width, LANES), F32),
            jax.ShapeDtypeStruct((pairs, HALO, LANES), F32),
        ),
        in_specs=[smem] + [vmem] * 6,
        out_specs=(vmem, vmem, vmem),
        scratch_shapes=[
            pltpu.VMEM((ROWS * wide, reference_feat.shape[2]), F32),
            pltpu.VMEM((reference_feat.shape[2], 2 * CH), F32),
            pltpu.VMEM((wide + 2 * HALO, LANES), F32),
            pltpu.VMEM((wide + 2 * HALO, LANES), F32),
            pltpu.VMEM((3 * (2 * RAD + 1), wide, LANES), F32),
        ],
        compiler_params=pltpu.CompilerParams(vmem_limit_bytes=24 << 20),
    )(place, reference_feat, secondary_feat, left, right, w_query_key, w_value)
    nexts = [passed_along(own, "tile", -step) for step in (1, 2, 3)]
    info = jnp.concatenate([
        jnp.concatenate([pair_offsets, before, after], axis=1).reshape(-1),
        jnp.stack([tile_id == 0, tile_id == count - 1]).astype(jnp.int32),
    ])
    result = pl.pallas_call(
        functools.partial(cost_kernel, pairs, width),
        out_shape=jax.ShapeDtypeStruct((width // 8, 8 * group), F32),
        in_specs=[smem] + [vmem] * 7,
        out_specs=vmem,
        scratch_shapes=[
            pltpu.VMEM((pairs, HALO + 4 * width + 16, LANES), F32),
            pltpu.VMEM((pairs, width + DISP + 16, LANES), F32),
            pltpu.VMEM((128, LANES), F32),
            pltpu.VMEM((DISP + 16, 8 * group), F32),
            pltpu.VMEM((pairs, DISP + 16, full), F32),
            pltpu.VMEM((3, pairs * DISP, full), BF16),
            pltpu.VMEM((3, pairs * DISP, full), BF16),
            pltpu.VMEM((2, 3, 10 * group, 8 * group), BF16),
            pltpu.VMEM((2, 3, 10 * group, 8 * group), BF16),
        ],
        compiler_params=pltpu.CompilerParams(vmem_limit_bytes=48 << 20),
    )(info, taps, feat, halo, own, *nexts)
    values = result.reshape(width // 8, 8, ROWS, GROUPS)[..., 0]
    return jnp.transpose(values, (2, 0, 1)).reshape(ROWS, width)


def solution(mesh):
    return jax.shard_map(
        on_device,
        mesh=mesh,
        in_specs=(
            P("groups", "tile", None),
            P("groups", None, "tile", None),
            P("groups", "tile"),
            P(),
            P(),
            P(),
            P(),
        ),
        out_specs=P("groups", "tile"),
        check_vma=False,
    )
```

```python
import functools

import jax
import jax.numpy as jnp
from jax import lax
from jax.experimental import pallas as pl
from jax.experimental.pallas import tpu as pltpu
from jax.sharding import PartitionSpec as P

GROUPS = 8
DISP = 128
RAD = 3
ROWS = 4
CH = 64
LANES = ROWS * CH
HALO = 8
F32 = jnp.float32
BF16 = jnp.bfloat16


def dot(a, b):
    return jnp.dot(a, b, preferred_element_type=F32)


def split2(x):
    hi = x.astype(BF16)
    return hi, (x - hi.astype(F32)).astype(BF16)


def split3(x):
    hi = x.astype(BF16)
    rest = x - hi.astype(F32)
    mid = rest.astype(BF16)
    return hi, mid, (rest - mid.astype(F32)).astype(BF16)


def attend_kernel(images, width, count, offsets, ref, sec, wq, wv,
                  out_ref, out_sec, out_halo, next0, next1, next2, before, after,
                  left, right, stacked, edges, weights, query, value, scores, send, recv):
    wide = width + 2 * HALO
    tile = lax.axis_index("tile")
    nexts = (next0, next1, next2)

    def present(step):
        return (tile + step >= 0) & (tile + step < count)

    def remote(source, target, place, step):
        return pltpu.make_async_remote_copy(
            src_ref=source, dst_ref=target, send_sem=send.at[place], recv_sem=recv.at[place],
            device_id={"tile": tile + step}, device_id_type=pl.DeviceIdType.MESH)

    barrier = pltpu.get_barrier_semaphore()
    partners = 0
    for step in (1, -1, 2, -2, 3, -3):
        @pl.when(present(step))
        def _(step=step):
            pl.semaphore_signal(barrier, inc=1, device_id={"tile": tile + step}, device_id_type=pl.DeviceIdType.MESH)

        partners = partners + jnp.where(present(step), 1, 0)
    pl.semaphore_wait(barrier, partners)

    tail = pl.ds(width - HALO, HALO)
    head = pl.ds(0, HALO)
    upward = [
        remote(ref.at[:, tail, :], left.at[0], 0, 1),
        remote(sec.at[:, :, tail, :], left.at[pl.ds(1, images - 1)], 1, 1),
        remote(offsets, before, 2, 1),
    ]
    downward = [
        remote(ref.at[:, head, :], right.at[0], 3, -1),
        remote(sec.at[:, :, head, :], right.at[pl.ds(1, images - 1)], 4, -1),
        remote(offsets, after, 5, -1),
    ]
    for step, copies in ((1, upward), (-1, downward)):
        @pl.when(present(step))
        def _(copies=copies):
            for copy in copies:
                copy.start()
    for step, halo, entry in ((-1, left, before), (1, right, after)):
        @pl.when(jnp.logical_not(present(step)))
        def _(halo=halo, entry=entry):
            halo[...] = jnp.zeros_like(halo)
            entry[...] = jnp.zeros_like(entry)
    for step, buffer in ((1, next0), (2, next1), (3, next2)):
        @pl.when(jnp.logical_not(present(step)))
        def _(buffer=buffer):
            buffer[...] = jnp.zeros_like(buffer)

    weights[:, :CH] = wq[...]
    weights[:, CH:] = wv[...]
    zeros = jnp.zeros((HALO, LANES), F32)
    for image in range(images):
        for row in range(ROWS):
            stacked[row * width:(row + 1) * width, :] = ref[row] if image == 0 else sec[image - 1, row]
        both = jnp.dot(stacked[...], weights[...], precision=lax.Precision.HIGHEST, preferred_element_type=F32)
        for row in range(ROWS):
            part = both[row * width:(row + 1) * width, :]
            query[image, 2 * HALO:2 * HALO + width, row * CH:(row + 1) * CH] = part[:, :CH]
            value[image, 2 * HALO:2 * HALO + width, row * CH:(row + 1) * CH] = part[:, CH:]
        for buffer in (query, value):
            buffer[image, 0:HALO, :] = zeros
            buffer[image, HALO + wide:, :] = zeros
    for step, copies in ((1, upward), (-1, downward)):
        @pl.when(present(step))
        def _(copies=copies):
            for copy in copies:
                copy.wait_send()

        @pl.when(present(-step))
        def _(copies=copies):
            for copy in copies:
                copy.wait_recv()
    for image in range(images):
        for row in range(ROWS):
            base = (image * ROWS + row) * 2 * HALO
            edges[base:base + HALO, :] = left[image, row]
            edges[base + HALO:base + 2 * HALO, :] = right[image, row]
    both = jnp.dot(edges[...], weights[...], precision=lax.Precision.HIGHEST, preferred_element_type=F32)
    for image in range(images):
        for row in range(ROWS):
            base = (image * ROWS + row) * 2 * HALO
            lanes = slice(row * CH, (row + 1) * CH)
            query[image, HALO:2 * HALO, lanes] = both[base:base + HALO, :CH]
            value[image, HALO:2 * HALO, lanes] = both[base:base + HALO, CH:]
            query[image, HALO + wide - HALO:HALO + wide, lanes] = both[base + HALO:base + 2 * HALO, :CH]
            value[image, HALO + wide - HALO:HALO + wide, lanes] = both[base + HALO:base + 2 * HALO, CH:]
    ones = jnp.where(
        lax.broadcasted_iota(jnp.int32, (LANES, LANES), 0) // CH
        == lax.broadcasted_iota(jnp.int32, (LANES, LANES), 1) // CH,
        1.0 / CH, 0.0).astype(BF16)

    def attention(image, length):
        lane_row = lax.broadcasted_iota(jnp.int32, (length, LANES), 1) // CH
        column = lax.broadcasted_iota(jnp.int32, (length, LANES), 0) + (tile * width - HALO)
        own = query[image, HALO:HALO + length, :]
        peak = jnp.full((length, LANES), -1e30, F32)
        place = 0
        for shift in range(-RAD, RAD + 1):
            keys = query[image, HALO + shift:HALO + shift + length, :]
            col_ok = (column + shift >= 0) & (column + shift < count * width)
            for step in (-1, 0, 1):
                moved = pltpu.roll(keys, (-step * CH) % LANES, 1) if step else keys
                hi, mid, low = split3(own * moved)
                score = dot(hi, ones) + dot(mid, ones) + dot(low, ones)
                row_ok = (lane_row + step >= 0) & (lane_row + step < ROWS)
                score = jnp.where(col_ok & row_ok, score, -1e30)
                scores[place, :length] = score
                peak = jnp.maximum(peak, score)
                place += 1
        total = jnp.zeros((length, LANES), F32)
        mixed = jnp.zeros((length, LANES), F32)
        place = 0
        for shift in range(-RAD, RAD + 1):
            vals = value[image, HALO + shift:HALO + shift + length, :]
            for step in (-1, 0, 1):
                moved = pltpu.roll(vals, (-step * CH) % LANES, 1) if step else vals
                weight = jnp.exp(scores[place, :length] - peak)
                total = total + weight
                mixed = mixed + weight * moved
                place += 1
        return column, value[image, HALO:HALO + length, :] + mixed / total

    sends = []
    for pair in range(images - 1):
        _, feature = attention(pair + 1, HALO + width)
        out_halo[pair] = feature[:HALO]
        out_sec[pair] = feature[HALO:]
        for step in (1, 2, 3):
            copy = remote(out_sec.at[pair], nexts[step - 1].at[pair], 6 + 3 * pair + step - 1, -step)
            sends.append((step, copy))

            @pl.when(present(-step))
            def _(copy=copy):
                copy.start()

    column, feature = attention(0, wide)
    out_ref[...] = jnp.where((column >= 0) & (column < count * width), feature, 0.0)
    for step, copy in sends:
        @pl.when(present(-step))
        def _(copy=copy):
            copy.wait_send()

        @pl.when(present(step))
        def _(copy=copy):
            copy.wait_recv()


def cost_kernel(pairs, width, info, taps, feat, halo, sec0, sec1, sec2, sec3, out,
                window, moved, padded, prod, plane, high, low, tail_high, tail_low, w_high, w_low, wt_high, wt_low, means):
    group = ROWS * GROUPS
    blocks = width // 8
    block = 8 * group
    edge_span = 2 * group
    full = (width + 4) * group
    tail = blocks * block
    tiles = DISP + 16
    window[...] = jnp.zeros_like(window)
    for pair in range(pairs):
        window[pair, 0:HALO, :] = halo[pair]
        for place, sec in enumerate((sec0, sec1, sec2, sec3)):
            window[pair, HALO + place * width:HALO + (place + 1) * width, :] = sec[pair]
        plane[pair, 0:8, :] = jnp.zeros((8, full), F32)
        plane[pair, 8 + DISP:, :] = jnp.zeros((8, full), F32)
    padded[...] = jnp.zeros_like(padded)
    padded[0:width + 2 * HALO, :] = feat[...]
    for conv in range(2):
        wt_high[conv] = jnp.zeros((block, block), BF16)
        wt_low[conv] = jnp.zeros((block, block), BF16)
        for tap in range(3):
            w_high[conv, tap] = jnp.zeros((block, block), BF16)
            w_low[conv, tap] = jnp.zeros((block, block), BF16)
            hi, lo = split2(taps[conv, tap])
            for col in range(8):
                lanes = slice(col * group, (col + 1) * group)
                inside = min(3, 8 - col) * group
                w_high[conv, tap, col * group:col * group + inside, lanes] = hi[:inside]
                w_low[conv, tap, col * group:col * group + inside, lanes] = lo[:inside]
                if inside < 3 * group:
                    base = tap * edge_span
                    wt_high[conv, base:base + 3 * group - inside, lanes] = hi[inside:]
                    wt_low[conv, base:base + 3 * group - inside, lanes] = lo[inside:]
    feat_hi, feat_lo = split2(padded[...].T)
    lane = lax.broadcasted_iota(jnp.int32, (DISP, 128), 1)

    def left_matrix(at):
        rows = lax.broadcasted_iota(jnp.int32, (128, block), 0)
        lanes = lax.broadcasted_iota(jnp.int32, (128, block), 1)
        spread = jnp.where(rows == lanes // group + (8 * at + HALO - 2), 1.0, 0.0).astype(BF16)
        keep = jnp.where(
            lax.broadcasted_iota(jnp.int32, (LANES, block), 0) // GROUPS
            == lax.broadcasted_iota(jnp.int32, (LANES, block), 1) % group,
            1.0 / (CH // GROUPS), 0.0)
        return (dot(feat_hi, spread) * keep).astype(BF16), (dot(feat_lo, spread) * keep).astype(BF16)

    def shifted(pair, offset, start, count):
        first = offset + (HALO - 2)
        rest = first % 8
        aligned = pl.multiple_of(first - rest + start, 8)
        rows = window[pair, pl.ds(aligned, count + 8), :]
        return pltpu.roll(rows, count + 8 - rest, 0)[:count]

    def skewed(rows, left_hi, left_lo, halves):
        right_hi, right_lo = split2(rows)
        prod[...] = dot(right_hi, left_hi) + dot(right_hi, left_lo) + dot(right_lo, left_hi)
        result = []
        for half in range(halves):
            lanes = slice(half * 128, (half + 1) * 128)
            value = prod[half * 4:half * 4 + DISP, lanes]
            for col in range(1, 4):
                other = prod[half * 4 + col:half * 4 + col + DISP, lanes]
                value = jnp.where(lane >= col * group, other, value)
            result.append(value)
        return result

    for pair in range(pairs):
        moved[pair] = shifted(pair, info[3 * pair], 0, width + tiles)

    def volume_step(at, carry):
        left_hi, left_lo = left_matrix(at)
        for pair in range(pairs):
            parts = skewed(moved[pair, pl.ds(pl.multiple_of(8 * at, 8), tiles), :], left_hi, left_lo, 2)
            for half in range(2):
                plane[pair, 8:8 + DISP, pl.ds(pl.multiple_of(at * block + half * 128, 128), 128)] = parts[half]
        return carry

    lax.fori_loop(0, blocks, volume_step, 0)
    left_hi, left_lo = left_matrix(0)
    for pair in range(pairs):
        (edge,) = skewed(shifted(pair, info[3 * pair + 1], 0, tiles), left_hi, left_lo, 1)
        plane[pair, 8:8 + DISP, 0:128] = jnp.where(lane < 2 * group, edge, plane[pair, 8:8 + DISP, 0:128])
    left_hi, left_lo = left_matrix(blocks)
    for pair in range(pairs):
        (mine,) = skewed(moved[pair, width:width + tiles, :], left_hi, left_lo, 1)
        (edge,) = skewed(shifted(pair, info[3 * pair + 2], width, tiles), left_hi, left_lo, 1)
        plane[pair, 8:8 + DISP, tail:tail + 128] = jnp.where(lane < 2 * group, mine, edge)

    def split_chunk(at, with_tail):
        lanes = pl.ds(pl.multiple_of(at * 128, 128), 128)
        for pair in range(pairs):
            rows = slice(pair * DISP, (pair + 1) * DISP)
            parts = [plane[pair, 7 + tap:7 + tap + DISP, lanes] for tap in range(3)]
            for tap in range(3):
                hi, lo = split2(parts[tap])
                high[tap, rows, lanes] = hi
                low[tap, rows, lanes] = lo
            if with_tail:
                base = pl.multiple_of(at * 128 - block, 128)
                mix = jnp.where(lane < edge_span, parts[0], pltpu.roll(parts[1], edge_span, 1))
                for place, part in ((0, split2(mix)), (128, (hi, lo))):
                    to = pl.ds(pl.multiple_of(base + place, 128), 128)
                    tail_high[rows, to] = part[0]
                    tail_low[rows, to] = part[1]

    def split_planes():
        split_chunk(0, False)
        split_chunk(1, False)

        def step(at, carry):
            split_chunk(2 * at, True)
            split_chunk(2 * at + 1, False)
            return carry

        lax.fori_loop(1, blocks, step, 0)
        split_chunk(2 * blocks, True)

    def conv(which, start):
        lanes = pl.ds(start, block)
        edge_hi = tail_high[:, lanes]
        total = dot(edge_hi, wt_high[which]) + dot(edge_hi, wt_low[which]) + dot(tail_low[:, lanes], wt_high[which])
        for tap in range(3):
            hi = high[tap, :, lanes]
            total = total + dot(hi, w_high[which, tap])
            total = total + dot(hi, w_low[which, tap])
            total = total + dot(low[tap, :, lanes], w_high[which, tap])
        return jnp.maximum(total, 0.0)

    def conv_end(which, start):
        lanes = pl.ds(start, 128)
        total = None
        for tap in range(3):
            hi = high[tap, :, lanes]
            wh = w_high[which, tap, 0:128, 0:128]
            wl = w_low[which, tap, 0:128, 0:128]
            term = dot(hi, wh) + dot(hi, wl) + dot(low[tap, :, lanes], wh)
            total = term if total is None else total + term
        return jnp.maximum(total, 0.0)

    split_planes()
    is_first, is_last = info[3 * pairs], info[3 * pairs + 1]

    def first_step(at, carry):
        start = pl.multiple_of(at * block, block)
        result = conv(0, start)
        lanes = lax.broadcasted_iota(jnp.int32, result.shape, 1)
        result = jnp.where((lanes < group) & (is_first + jnp.where(at == 0, 1, 0) == 2), 0.0, result)
        for pair in range(pairs):
            plane[pair, 8:8 + DISP, pl.ds(start, block)] = result[pair * DISP:(pair + 1) * DISP]
        return carry

    lax.fori_loop(0, blocks, first_step, 0)
    result = conv_end(0, tail)
    lanes = lax.broadcasted_iota(jnp.int32, result.shape, 1)
    result = jnp.where((lanes >= group) & (is_last == 1), 0.0, result)
    for pair in range(pairs):
        plane[pair, 8:8 + DISP, tail:tail + 128] = result[pair * DISP:(pair + 1) * DISP]
    split_planes()
    level = lax.broadcasted_iota(jnp.int32, (DISP, block), 0).astype(F32)

    def second_step(at, carry):
        result = conv(1, pl.multiple_of(at * block, block))
        score = result[:DISP]
        for pair in range(1, pairs):
            score = score + result[pair * DISP:(pair + 1) * DISP]
        for shift in (4, 2, 1):
            score = score + pltpu.roll(score, block - shift, 1)
        weight = jnp.exp(score - jnp.max(score, axis=0, keepdims=True))
        mean = jnp.sum(weight * level, axis=0, keepdims=True) / jnp.sum(weight, axis=0, keepdims=True)
        means[pl.ds(at, 1), :] = mean / DISP
        return carry

    lax.fori_loop(0, blocks, second_step, 0)
    own_row = lax.broadcasted_iota(jnp.int32, (8, block), 0) * GROUPS
    own_row = own_row == lax.broadcasted_iota(jnp.int32, (8, block), 1) % group
    from_lane = lax.broadcasted_iota(jnp.int32, (block, width), 0) // group
    to_col = lax.broadcasted_iota(jnp.int32, (block, width), 1)
    total = jnp.zeros((8, width), F32)
    for at in range(blocks):
        pick = jnp.where(from_lane + 8 * at == to_col, 1.0, 0.0).astype(BF16)
        for part in split3(jnp.where(own_row, jnp.broadcast_to(means[at:at + 1, :], (8, block)), 0.0)):
            total = total + dot(part, pick)
    out[...] = total[:ROWS]


def exchange(pairs, width, count, features):
    images = pairs + 1
    wide = width + 2 * HALO
    vmem = pl.BlockSpec(memory_space=pltpu.VMEM)
    shifted = jax.ShapeDtypeStruct((pairs, width, LANES), F32)
    entry = jax.ShapeDtypeStruct((pairs, 128), jnp.int32)
    copies = 6 + 3 * pairs

    def ordered(*args):
        feat, own, halo, next0, next1, next2, before, after = call(*args)
        return feat, halo, own, next0, next1, next2, before, after

    call = pl.pallas_call(
        functools.partial(attend_kernel, images, width, count),
        out_shape=(
            jax.ShapeDtypeStruct((wide, LANES), F32),
            shifted,
            jax.ShapeDtypeStruct((pairs, HALO, LANES), F32),
            shifted, shifted, shifted, entry, entry,
        ),
        in_specs=[vmem] * 5,
        out_specs=(vmem,) * 8,
        scratch_shapes=[
            pltpu.VMEM((images, ROWS, HALO, features), F32),
            pltpu.VMEM((images, ROWS, HALO, features), F32),
            pltpu.VMEM((ROWS * width, features), F32),
            pltpu.VMEM((images * ROWS * 2 * HALO, features), F32),
            pltpu.VMEM((features, 2 * CH), F32),
            pltpu.VMEM((images, wide + 2 * HALO, LANES), F32),
            pltpu.VMEM((images, wide + 2 * HALO, LANES), F32),
            pltpu.VMEM((3 * (2 * RAD + 1), wide, LANES), F32),
            pltpu.SemaphoreType.DMA((copies,)),
            pltpu.SemaphoreType.DMA((copies,)),
        ],
        compiler_params=pltpu.CompilerParams(
            vmem_limit_bytes=24 << 20, collective_id=0, has_side_effects=True),
    )
    return ordered


def tap_matrices(conv_first, conv_second):
    both = jnp.stack([conv_first, conv_second])
    flipped = jnp.transpose(both, (0, 5, 4, 3, 2, 1))
    rows = jnp.pad(flipped, ((0, 0), (0, 0), (0, 0), (ROWS - 1, ROWS - 1), (0, 0), (0, 0)))
    parts = [rows[:, :, :, ROWS - out:2 * ROWS - out] for out in range(ROWS)]
    joined = jnp.concatenate(parts, axis=-1)
    return joined.reshape(2, 3, 3 * ROWS * GROUPS, ROWS * GROUPS)


def on_device(reference_feat, secondary_feat, pair_offsets, w_query_key, w_value, conv_first, conv_second):
    pairs = secondary_feat.shape[0]
    width = reference_feat.shape[1]
    tile_id = lax.axis_index("tile")
    count = lax.axis_size("tile")
    group = ROWS * GROUPS
    full = (width + 4) * group
    vmem = pl.BlockSpec(memory_space=pltpu.VMEM)
    smem = pl.BlockSpec(memory_space=pltpu.SMEM)
    features = reference_feat.shape[2]
    entries = jnp.broadcast_to(pair_offsets, (pairs, 128))
    taps = tap_matrices(conv_first, conv_second)
    feat, halo, own, next0, next1, next2, before, after = exchange(
        pairs, width, lax.axis_size("tile"), features)(entries, reference_feat, secondary_feat, w_query_key, w_value)
    info = jnp.concatenate([
        jnp.concatenate([pair_offsets, before[:, :1], after[:, :1]], axis=1).reshape(-1),
        jnp.stack([tile_id == 0, tile_id == count - 1]).astype(jnp.int32),
    ])
    return pl.pallas_call(
        functools.partial(cost_kernel, pairs, width),
        out_shape=jax.ShapeDtypeStruct((ROWS, width), F32),
        in_specs=[smem] + [vmem] * 7,
        out_specs=vmem,
        scratch_shapes=[
            pltpu.VMEM((pairs, HALO + 4 * width + 16, LANES), F32),
            pltpu.VMEM((pairs, width + DISP + 16, LANES), F32),
            pltpu.VMEM((128, LANES), F32),
            pltpu.VMEM((DISP + 16, 8 * group), F32),
            pltpu.VMEM((pairs, DISP + 16, full), F32),
            pltpu.VMEM((3, pairs * DISP, full), BF16),
            pltpu.VMEM((3, pairs * DISP, full), BF16),
            pltpu.VMEM((pairs * DISP, width * group), BF16),
            pltpu.VMEM((pairs * DISP, width * group), BF16),
            pltpu.VMEM((2, 3, 8 * group, 8 * group), BF16),
            pltpu.VMEM((2, 3, 8 * group, 8 * group), BF16),
            pltpu.VMEM((2, 8 * group, 8 * group), BF16),
            pltpu.VMEM((2, 8 * group, 8 * group), BF16),
            pltpu.VMEM((width // 8, 8 * group), F32),
        ],
        compiler_params=pltpu.CompilerParams(vmem_limit_bytes=48 << 20),
    )(info, taps, feat, halo, own, next0, next1, next2)


def solution(mesh):
    return jax.shard_map(
        on_device,
        mesh=mesh,
        in_specs=(
            P("groups", "tile", None),
            P("groups", None, "tile", None),
            P("groups", "tile"),
            P(),
            P(),
            P(),
            P(),
        ),
        out_specs=P("groups", "tile"),
        check_vma=False,
    )
```

```python
import functools
from functools import reduce

import jax
import jax.numpy as jnp
from jax import lax
from jax.experimental import pallas as pl
from jax.experimental.pallas import tpu as pltpu
from jax.sharding import PartitionSpec as P

GROUPS = 8
DISP = 128
RAD = 3
ROWS = 4
CH = 64
LANES = ROWS * CH
HALO = 8
F32 = jnp.float32
BF16 = jnp.bfloat16


def dot(a, b):
    return jnp.dot(a, b, preferred_element_type=F32)


def aligned(start):
    return start if isinstance(start, int) else pl.multiple_of(start, 128)


def split2(x):
    hi = x.astype(BF16)
    return hi, (x - hi.astype(F32)).astype(BF16)


def split3(x):
    hi = x.astype(BF16)
    rest = x - hi.astype(F32)
    mid = rest.astype(BF16)
    return hi, mid, (rest - mid.astype(F32)).astype(BF16)


def attend_kernel(images, width, count, offsets, ref, sec, wq, wv,
                  out_ref, out_sec, out_halo, next0, next1, next2, before, after,
                  left, right, stacked, edges, weights, query, value, scores, send, recv):
    wide = width + 2 * HALO
    tile = lax.axis_index("tile")
    nexts = (next0, next1, next2)

    def present(step):
        return (tile + step >= 0) & (tile + step < count)

    def remote(source, target, place, step):
        return pltpu.make_async_remote_copy(
            src_ref=source, dst_ref=target, send_sem=send.at[place], recv_sem=recv.at[place],
            device_id={"tile": tile + step}, device_id_type=pl.DeviceIdType.MESH)

    barrier = pltpu.get_barrier_semaphore()
    partners = 0
    for step in (1, -1, 3, -3):
        @pl.when(present(step))
        def _(step=step):
            pl.semaphore_signal(barrier, inc=1, device_id={"tile": tile + step}, device_id_type=pl.DeviceIdType.MESH)

        partners = partners + jnp.where(present(step), 1, 0)
    pl.semaphore_wait(barrier, partners)

    tail = pl.ds(width - HALO, HALO)
    head = pl.ds(0, HALO)
    upward = [
        remote(ref.at[:, tail, :], left.at[0], 0, 1),
        remote(sec.at[:, :, tail, :], left.at[pl.ds(1, images - 1)], 1, 1),
        remote(offsets, before, 2, 1),
    ]
    downward = [
        remote(ref.at[:, head, :], right.at[0], 3, -1),
        remote(sec.at[:, :, head, :], right.at[pl.ds(1, images - 1)], 4, -1),
        remote(offsets, after, 5, -1),
    ]
    for step, copies in ((1, upward), (-1, downward)):
        @pl.when(present(step))
        def _(copies=copies):
            for copy in copies:
                copy.start()
    for step, halo, entry in ((-1, left, before), (1, right, after)):
        @pl.when(jnp.logical_not(present(step)))
        def _(halo=halo, entry=entry):
            halo[...] = jnp.zeros_like(halo)
            entry[...] = jnp.zeros_like(entry)
    for step, buffer in ((1, next0), (2, next1), (3, next2)):
        @pl.when(jnp.logical_not(present(step)))
        def _(buffer=buffer):
            buffer[...] = jnp.zeros_like(buffer)

    weights[:, :CH] = wq[...]
    weights[:, CH:] = wv[...]
    zeros = jnp.zeros((HALO, LANES), F32)
    for image in range(images):
        for row in range(ROWS):
            stacked[row * width:(row + 1) * width, :] = ref[row] if image == 0 else sec[image - 1, row]
        both = jnp.dot(stacked[...], weights[...], precision=lax.Precision.HIGHEST, preferred_element_type=F32)
        for row in range(ROWS):
            part = both[row * width:(row + 1) * width, :]
            query[image, 2 * HALO:2 * HALO + width, row * CH:(row + 1) * CH] = part[:, :CH]
            value[image, 2 * HALO:2 * HALO + width, row * CH:(row + 1) * CH] = part[:, CH:]
        for buffer in (query, value):
            buffer[image, 0:HALO, :] = zeros
            buffer[image, HALO + wide:, :] = zeros
    for step, copies in ((1, upward), (-1, downward)):
        @pl.when(present(step))
        def _(copies=copies):
            for copy in copies:
                copy.wait_send()

        @pl.when(present(-step))
        def _(copies=copies):
            for copy in copies:
                copy.wait_recv()
    for image in range(images):
        for row in range(ROWS):
            base = (image * ROWS + row) * 2 * HALO
            edges[base:base + HALO, :] = left[image, row]
            edges[base + HALO:base + 2 * HALO, :] = right[image, row]
    both = jnp.dot(edges[...], weights[...], precision=lax.Precision.HIGHEST, preferred_element_type=F32)
    for image in range(images):
        for row in range(ROWS):
            base = (image * ROWS + row) * 2 * HALO
            lanes = slice(row * CH, (row + 1) * CH)
            query[image, HALO:2 * HALO, lanes] = both[base:base + HALO, :CH]
            value[image, HALO:2 * HALO, lanes] = both[base:base + HALO, CH:]
            query[image, HALO + wide - HALO:HALO + wide, lanes] = both[base + HALO:base + 2 * HALO, :CH]
            value[image, HALO + wide - HALO:HALO + wide, lanes] = both[base + HALO:base + 2 * HALO, CH:]
    ones = jnp.where(
        lax.broadcasted_iota(jnp.int32, (LANES, LANES), 0) // CH
        == lax.broadcasted_iota(jnp.int32, (LANES, LANES), 1) // CH,
        1.0 / CH, 0.0).astype(BF16)

    def attention(image, length):
        lane_row = lax.broadcasted_iota(jnp.int32, (length, LANES), 1) // CH
        column = lax.broadcasted_iota(jnp.int32, (length, LANES), 0) + (tile * width - HALO)
        own = query[image, HALO:HALO + length, :]
        peak = jnp.full((length, LANES), -1e30, F32)
        place = 0
        for shift in range(-RAD, RAD + 1):
            keys = query[image, HALO + shift:HALO + shift + length, :]
            col_ok = (column + shift >= 0) & (column + shift < count * width)
            for step in (-1, 0, 1):
                moved = pltpu.roll(keys, (-step * CH) % LANES, 1) if step else keys
                hi, mid, low = split3(own * moved)
                score = dot(hi, ones) + dot(mid, ones) + dot(low, ones)
                row_ok = (lane_row + step >= 0) & (lane_row + step < ROWS)
                score = jnp.where(col_ok & row_ok, score, -1e30)
                scores[place, :length] = score
                peak = jnp.maximum(peak, score)
                place += 1
        total = jnp.zeros((length, LANES), F32)
        mixed = jnp.zeros((length, LANES), F32)
        place = 0
        for shift in range(-RAD, RAD + 1):
            vals = value[image, HALO + shift:HALO + shift + length, :]
            for step in (-1, 0, 1):
                moved = pltpu.roll(vals, (-step * CH) % LANES, 1) if step else vals
                weight = jnp.exp(scores[place, :length] - peak)
                total = total + weight
                mixed = mixed + weight * moved
                place += 1
        return column, value[image, HALO:HALO + length, :] + mixed / total

    sends = []
    for pair in range(images - 1):
        _, feature = attention(pair + 1, HALO + width)
        out_halo[pair] = feature[:HALO]
        out_sec[pair] = feature[HALO:]
        for step in (1, 3):
            copy = remote(out_sec.at[pair], nexts[step - 1].at[pair], 6 + 3 * pair + step - 1, -step)
            sends.append((step, copy))

            @pl.when(present(-step))
            def _(copy=copy):
                copy.start()

    column, feature = attention(0, wide)
    out_ref[...] = jnp.where((column >= 0) & (column < count * width), feature, 0.0)
    odd = tile % 2 == 1
    forwards = []
    for step, copy in sends:
        @pl.when(present(step))
        def _(copy=copy):
            copy.wait_recv()

        pair = len(forwards) // 2
        source, offset, chosen = (next0, -1, odd) if step == 1 else (next2, 1, jnp.logical_not(odd))
        forward = remote(source.at[pair], next1.at[pair], 7 + 3 * pair, offset)
        going = chosen & present(step)
        forwards.append((going, forward))

        @pl.when(going)
        def _(forward=forward):
            forward.start()

    for step, copy in sends:
        @pl.when(present(-step))
        def _(copy=copy):
            copy.wait_send()

    for going, forward in forwards:
        @pl.when(going)
        def _(forward=forward):
            forward.wait_send()

    for _, forward in forwards[::2]:
        @pl.when(present(2))
        def _(forward=forward):
            forward.wait_recv()


def cost_kernel(pairs, width, info, taps, feat, halo, sec0, sec1, sec2, sec3, out,
                window, moved, padded, prod, keep, gap, side, high, low, ends, w_high, w_low, w_ends, means):
    group = ROWS * GROUPS
    blocks = width // 8
    block = 8 * group
    edge_span = 2 * group
    tail = blocks * block
    tiles = DISP + 16
    window[:, HALO + 4 * width:, :] = jnp.zeros((pairs, 16, LANES), F32)
    for pair in range(pairs):
        window[pair, 0:HALO, :] = halo[pair]
        for place, sec in enumerate((sec0, sec1, sec2, sec3)):
            window[pair, HALO + place * width:HALO + (place + 1) * width, :] = sec[pair]
        for place in range(2):
            side[place, pair, 0:8, :] = jnp.zeros((8, block), F32)
            side[place, pair, 8 + DISP:, :] = jnp.zeros((8, block), F32)
    padded[...] = jnp.zeros_like(padded)
    padded[0:width + 2 * HALO, :] = feat[...]
    for conv in range(2):
        for tap in range(3):
            w_high[conv, tap] = jnp.zeros((block, block), BF16)
            w_low[conv, tap] = jnp.zeros((block, block), BF16)
            w_ends[conv, tap] = jnp.zeros((block, block), BF16)
            hi, lo = split2(taps[conv, tap])
            for col in range(8):
                lanes = slice(col * group, (col + 1) * group)
                inside = min(3, 8 - col) * group
                rest = 3 * group - inside
                w_high[conv, tap, col * group:col * group + inside, lanes] = hi[:inside]
                w_low[conv, tap, col * group:col * group + inside, lanes] = lo[:inside]
                if rest:
                    w_ends[conv, tap, 0:rest, lanes] = hi[inside:]
                    w_ends[conv, tap, edge_span:edge_span + rest, lanes] = hi[inside:]
                    w_ends[conv, tap, 2 * edge_span:2 * edge_span + rest, lanes] = lo[inside:]
    lanes = lax.broadcasted_iota(jnp.int32, (128, block), 1)
    gap[...] = lax.broadcasted_iota(jnp.int32, (128, block), 0) - (lanes >> 5)
    keep[...] = jnp.where(
        lax.broadcasted_iota(jnp.int32, (LANES, block), 0) >> 3
        == (lax.broadcasted_iota(jnp.int32, (LANES, block), 1) & (group - 1)),
        1.0 / (CH // GROUPS), 0.0)
    feat_hi, feat_lo = split2(padded[...].T)
    lane = lax.broadcasted_iota(jnp.int32, (DISP, 128), 1)

    def left_matrix(at):
        spread = jnp.where(gap[...] == 8 * at + (HALO - 2), 1.0, 0.0).astype(BF16)
        return (dot(feat_hi, spread) * keep[...]).astype(BF16), (dot(feat_lo, spread) * keep[...]).astype(BF16)

    def shifted(pair, offset, start, count):
        first = offset + (HALO - 2)
        rest = first % 8
        base = pl.multiple_of(first - rest + start, 8)
        rows = window[pair, pl.ds(base, count + 8), :]
        return pltpu.roll(rows, count + 8 - rest, 0)[:count]

    def skewed(rows, left_hi, left_lo, halves):
        right_hi, right_lo = split2(rows)
        prod[...] = dot(right_hi, left_hi) + dot(right_hi, left_lo) + dot(right_lo, left_hi)
        result = []
        for half in range(halves):
            lanes = slice(half * 128, (half + 1) * 128)
            value = prod[half * 4:half * 4 + DISP, lanes]
            for col in range(1, 4):
                other = prod[half * 4 + col:half * 4 + col + DISP, lanes]
                value = jnp.where(lane >= col * group, other, value)
            result.append(value)
        return result

    for pair in range(pairs):
        moved[pair] = shifted(pair, info[3 * pair], 0, width + tiles)

    def keep_first(pair, at, value):
        rows = slice(pair * DISP, (pair + 1) * DISP)
        start = at * block
        hi, lo = split2(value)
        mix = jnp.where(lane < edge_span, hi.astype(F32), pltpu.roll(lo.astype(F32), edge_span, 1))
        high[rows, pl.ds(aligned(start), 128)] = hi
        low[rows, pl.ds(aligned(start), 128)] = lo
        ends[rows, pl.ds(aligned(start), 128)] = mix.astype(BF16)
        ends[rows, pl.ds(aligned(start + 128), 128)] = hi

    def keep_second(pair, at, value):
        rows = slice(pair * DISP, (pair + 1) * DISP)
        hi, lo = split2(value)
        high[rows, pl.ds(aligned(at * block + 128), 128)] = hi
        low[rows, pl.ds(aligned(at * block + 128), 128)] = lo

    def volume_step(at, carry):
        left_hi, left_lo = left_matrix(at)
        for pair in range(pairs):
            parts = skewed(moved[pair, pl.ds(pl.multiple_of(8 * at, 8), tiles), :], left_hi, left_lo, 2)
            keep_first(pair, at, parts[0])
            keep_second(pair, at, parts[1])
        return carry

    lax.fori_loop(1, blocks, volume_step, 0)
    left_hi, left_lo = left_matrix(0)
    for pair in range(pairs):
        mine, second = skewed(moved[pair, 0:tiles, :], left_hi, left_lo, 2)
        (edge,) = skewed(shifted(pair, info[3 * pair + 1], 0, tiles), left_hi, left_lo, 1)
        keep_first(pair, 0, jnp.where(lane < 2 * group, edge, mine))
        keep_second(pair, 0, second)
    left_hi, left_lo = left_matrix(blocks)
    for pair in range(pairs):
        (mine,) = skewed(moved[pair, width:width + tiles, :], left_hi, left_lo, 1)
        (edge,) = skewed(shifted(pair, info[3 * pair + 2], width, tiles), left_hi, left_lo, 1)
        keep_first(pair, blocks, jnp.where(lane < 2 * group, mine, edge))

    def joined(products, count):
        for place in range(2):
            for pair in range(pairs):
                side[place, pair, 8:8 + DISP, 0:count] = products[2 * place][pair * DISP:(pair + 1) * DISP]
        return [
            jnp.maximum(
                side[0, pair, 7:7 + DISP, 0:count] + products[1][pair * DISP:(pair + 1) * DISP]
                + side[1, pair, 9:9 + DISP, 0:count], 0.0)
            for pair in range(pairs)
        ]

    def conv(which, at):
        hi = high[:, pl.ds(aligned(at * block), block)]
        lo = low[:, pl.ds(aligned(at * block), block)]
        end = ends[:, pl.ds(aligned(at * block + block), block)]
        return joined([
            dot(hi, w_high[which, tap]) + dot(hi, w_low[which, tap])
            + dot(lo, w_high[which, tap]) + dot(end, w_ends[which, tap])
            for tap in range(3)
        ], block)

    def conv_end(which):
        hi = high[:, tail:tail + 128]
        lo = low[:, tail:tail + 128]
        return joined([
            dot(hi, w_high[which, tap, 0:128, 0:128]) + dot(hi, w_low[which, tap, 0:128, 0:128])
            + dot(lo, w_high[which, tap, 0:128, 0:128])
            for tap in range(3)
        ], 128)

    is_first, is_last = info[3 * pairs], info[3 * pairs + 1]

    def first_step(at, carry):
        results = conv(0, at)
        for pair in range(pairs):
            first = results[pair][:, :128]
            outside = is_first + jnp.where(at == 0, 1, 0) == 2
            keep_first(pair, at, jnp.where((lane < group) & outside, 0.0, first))
            keep_second(pair, at, results[pair][:, 128:])
        return carry

    lax.fori_loop(0, blocks, first_step, 0)
    results = conv_end(0)
    for pair in range(pairs):
        keep_first(pair, blocks, jnp.where((lane >= group) & (is_last == 1), 0.0, results[pair]))
    level = lax.broadcasted_iota(jnp.int32, (DISP, block), 0).astype(F32)

    def second_step(at, carry):
        score = reduce(jnp.add, conv(1, at))
        for shift in (4, 2, 1):
            score = score + pltpu.roll(score, block - shift, 1)
        weight = jnp.exp(score - jnp.max(score, axis=0, keepdims=True))
        mean = jnp.sum(weight * level, axis=0, keepdims=True) / jnp.sum(weight, axis=0, keepdims=True)
        means[pl.ds(at, 1), :] = mean / DISP
        return carry

    lax.fori_loop(0, blocks, second_step, 0)
    own_row = lax.broadcasted_iota(jnp.int32, (8, block), 0) * GROUPS
    own_row = own_row == lax.broadcasted_iota(jnp.int32, (8, block), 1) % group
    from_lane = lax.broadcasted_iota(jnp.int32, (block, width), 0) // group
    to_col = lax.broadcasted_iota(jnp.int32, (block, width), 1)
    total = jnp.zeros((8, width), F32)
    for at in range(blocks):
        pick = jnp.where(from_lane + 8 * at == to_col, 1.0, 0.0).astype(BF16)
        for part in split3(jnp.where(own_row, jnp.broadcast_to(means[at:at + 1, :], (8, block)), 0.0)):
            total = total + dot(part, pick)
    out[...] = total[:ROWS]


def exchange(pairs, width, count, features):
    images = pairs + 1
    wide = width + 2 * HALO
    vmem = pl.BlockSpec(memory_space=pltpu.VMEM)
    shifted = jax.ShapeDtypeStruct((pairs, width, LANES), F32)
    entry = jax.ShapeDtypeStruct((pairs, 128), jnp.int32)
    copies = 6 + 3 * pairs

    def ordered(*args):
        feat, own, halo, next0, next1, next2, before, after = call(*args)
        return feat, halo, own, next0, next1, next2, before, after

    call = pl.pallas_call(
        functools.partial(attend_kernel, images, width, count),
        out_shape=(
            jax.ShapeDtypeStruct((wide, LANES), F32),
            shifted,
            jax.ShapeDtypeStruct((pairs, HALO, LANES), F32),
            shifted, shifted, shifted, entry, entry,
        ),
        in_specs=[vmem] * 5,
        out_specs=(vmem,) * 8,
        scratch_shapes=[
            pltpu.VMEM((images, ROWS, HALO, features), F32),
            pltpu.VMEM((images, ROWS, HALO, features), F32),
            pltpu.VMEM((ROWS * width, features), F32),
            pltpu.VMEM((images * ROWS * 2 * HALO, features), F32),
            pltpu.VMEM((features, 2 * CH), F32),
            pltpu.VMEM((images, wide + 2 * HALO, LANES), F32),
            pltpu.VMEM((images, wide + 2 * HALO, LANES), F32),
            pltpu.VMEM((3 * (2 * RAD + 1), wide, LANES), F32),
            pltpu.SemaphoreType.DMA((copies,)),
            pltpu.SemaphoreType.DMA((copies,)),
        ],
        compiler_params=pltpu.CompilerParams(
            vmem_limit_bytes=24 << 20, collective_id=0, has_side_effects=True),
    )
    return ordered


def tap_matrices(conv_first, conv_second):
    both = jnp.stack([conv_first, conv_second])
    flipped = jnp.transpose(both, (0, 5, 4, 3, 2, 1))
    rows = jnp.pad(flipped, ((0, 0), (0, 0), (0, 0), (ROWS - 1, ROWS - 1), (0, 0), (0, 0)))
    parts = [rows[:, :, :, ROWS - out:2 * ROWS - out] for out in range(ROWS)]
    joined = jnp.concatenate(parts, axis=-1)
    return joined.reshape(2, 3, 3 * ROWS * GROUPS, ROWS * GROUPS)


def on_device(reference_feat, secondary_feat, pair_offsets, w_query_key, w_value, conv_first, conv_second):
    pairs = secondary_feat.shape[0]
    width = reference_feat.shape[1]
    tile_id = lax.axis_index("tile")
    count = lax.axis_size("tile")
    group = ROWS * GROUPS
    full = (width + 8) * group
    vmem = pl.BlockSpec(memory_space=pltpu.VMEM)
    smem = pl.BlockSpec(memory_space=pltpu.SMEM)
    features = reference_feat.shape[2]
    entries = jnp.broadcast_to(pair_offsets, (pairs, 128))
    taps = tap_matrices(conv_first, conv_second)
    feat, halo, own, next0, next1, next2, before, after = exchange(
        pairs, width, lax.axis_size("tile"), features)(entries, reference_feat, secondary_feat, w_query_key, w_value)
    info = jnp.concatenate([
        jnp.concatenate([pair_offsets, before[:, :1], after[:, :1]], axis=1).reshape(-1),
        jnp.stack([tile_id == 0, tile_id == count - 1]).astype(jnp.int32),
    ])
    return pl.pallas_call(
        functools.partial(cost_kernel, pairs, width),
        out_shape=jax.ShapeDtypeStruct((ROWS, width), F32),
        in_specs=[smem] + [vmem] * 7,
        out_specs=vmem,
        scratch_shapes=[
            pltpu.VMEM((pairs, HALO + 4 * width + 16, LANES), F32),
            pltpu.VMEM((pairs, width + DISP + 16, LANES), F32),
            pltpu.VMEM((128, LANES), F32),
            pltpu.VMEM((DISP + 16, 8 * group), F32),
            pltpu.VMEM((LANES, 8 * group), F32),
            pltpu.VMEM((128, 8 * group), jnp.int32),
            pltpu.VMEM((2, pairs, DISP + 16, 8 * group), F32),
            pltpu.VMEM((pairs * DISP, full), BF16),
            pltpu.VMEM((pairs * DISP, full), BF16),
            pltpu.VMEM((pairs * DISP, full), BF16),
            pltpu.VMEM((2, 3, 8 * group, 8 * group), BF16),
            pltpu.VMEM((2, 3, 8 * group, 8 * group), BF16),
            pltpu.VMEM((2, 3, 8 * group, 8 * group), BF16),
            pltpu.VMEM((width // 8, 8 * group), F32),
        ],
        compiler_params=pltpu.CompilerParams(vmem_limit_bytes=48 << 20),
    )(info, taps, feat, halo, own, next0, next1, next2)


def solution(mesh):
    return jax.shard_map(
        on_device,
        mesh=mesh,
        in_specs=(
            P("groups", "tile", None),
            P("groups", None, "tile", None),
            P("groups", "tile"),
            P(),
            P(),
            P(),
            P(),
        ),
        out_specs=P("groups", "tile"),
        check_vma=False,
    )
```
